128 devices in a mesh: row: 8 (over y, core), col: 16 (over z, x).
Axes of the slice: x: 4, y: 4, z: 4, core: 2. Of those that a mesh axis runs over, the one named last changes fastest.
Arguments:
- amplitudes: bfloat16 [16, 16, 4, 128, 128], P('row', 'col'), may hold values from -6 to 6
- cholesky: bfloat16 [16, 16, 10, 128, 128], P('row', 'col'), may hold values from -0.5 to 0.5, as said below
- tile_mask: int32 [16, 16], P('row', 'col'), may hold values 0 or 1
Outputs:
- antisymmetrized: bfloat16 [16, 16, 4, 128, 128], P('row', 'col')
The draws below stay inside these ranges and needn't reach their ends.
Inputs may be any that keep to these rules, and one draw needn't show every extreme that they name: cholesky is symmetric: cholesky[a,c,q,x,u] equals cholesky[c,a,q,u,x].
All inputs are finite; a program needn't handle non-finite values. No bound on the sum of `tile_mask` on one device may be relied on, other than what follows from the above.
Results may differ from the reference program's by a relative error of at most 0.0059.
Values may be sent and summed in bfloat16 or wider, within the bound.
A program may use at most 128 MiB of HBM per device.

```python
import jax
import jax.numpy as jnp
from jax import lax

TILE = 128
NT = 16
OCC = 2
PAIRS = 4
NQ = 10


def draw_cholesky(key, part):
    array_shape = (NT, NT, NQ, TILE, TILE)
    samples = jnp.clip(jax.random.normal(key, array_shape, jnp.float32), -4.0, 4.0)
    symmetric = (samples + jnp.transpose(samples, (1, 0, 2, 4, 3))) * 0.70710678
    factor = (NT * TILE) ** (-0.5) * (NQ / 2.0) ** (-0.25)
    return (symmetric * factor).astype(jnp.bfloat16)


def plant(values, key, low, top_value):
    longest = values.shape.index(max(values.shape))
    spots = []
    for shift in (0, 1):
        where = [jax.random.randint(jax.random.fold_in(key, axis), (), 0, length) for axis, length in enumerate(values.shape)]
        where[longest] = (where[longest] + shift) % values.shape[longest]
        spots.append(tuple(where))
    return values.at[spots[0]].set(low).at[spots[1]].set(top_value)


def level_of(key, extent, cuts, smallest, top_value):
    loudness, own = 1.0, jax.random.fold_in(key, 6)
    for axis_at, parts in cuts:
        heights = jnp.exp(jax.random.uniform(jax.random.fold_in(own, axis_at), (parts,), jnp.float32, smallest / len(cuts), top_value / len(cuts)))
        loudness = loudness * jnp.repeat(heights, extent[axis_at] // parts).reshape([-1 if axis == axis_at else 1 for axis in range(len(extent))])
    return loudness


def gaussian(own_key, extent, spread, bound, split=(), held_as=jnp.bfloat16):
    array = spread * jax.random.normal(own_key, extent, jnp.float32)
    if split:
        array = array * level_of(own_key, extent, split, -0.22, 0.18)
    return jnp.clip(array, -bound, bound).astype(held_as)


def setup_inputs(seed: int = 0) -> dict:
    arg_keys = jax.random.split(jax.random.key(seed), 4)
    return {
        "amplitudes": gaussian(arg_keys[0], (NT, NT, PAIRS, TILE, TILE), 1.0, 6.0, ((0, 8), (1, 16))),
        "cholesky": draw_cholesky(jax.random.fold_in(arg_keys[3], 71), 0),
        "tile_mask": plant((jax.random.randint(arg_keys[2], (NT, NT), 0, 2) < 1).astype(jnp.int32), jax.random.fold_in(arg_keys[2], 1), 0, 1),
    }


def reference(amplitudes, cholesky, tile_mask):
    weights = cholesky.astype(jnp.float32)
    masked = amplitudes.astype(jnp.float32) * tile_mask.astype(jnp.float32)[:, :, None, None, None]

    def one_column(position):
        column = lax.dynamic_index_in_dim(weights, position, 0, keepdims=False)
        halves = jnp.einsum("cdpuv,dqyv->cpuqy", masked, column)
        halves = lax.optimization_barrier(halves.astype(jnp.bfloat16)).astype(jnp.float32)
        return jnp.einsum("acqxu,cpuqy->apxy", weights, halves)

    ladder = lax.map(one_column, jnp.arange(NT, dtype=jnp.int32))
    ladder = jnp.transpose(ladder, (1, 0, 2, 3, 4))
    rounded = lax.optimization_barrier(ladder.astype(jnp.bfloat16)).astype(jnp.float32)
    mirror = jnp.transpose(rounded, (1, 0, 2, 4, 3)).reshape(NT, NT, OCC, OCC, TILE, TILE)
    mirror = jnp.transpose(mirror, (0, 1, 3, 2, 4, 5)).reshape(NT, NT, PAIRS, TILE, TILE)
    return (rounded - mirror).astype(jnp.bfloat16)
```

```python
import jax
import jax.numpy as jnp
from jax import lax
from jax.experimental import pallas as pl
from jax.experimental.pallas import tpu as pltpu
from jax.sharding import PartitionSpec as P

MESH = pl.DeviceIdType.MESH
BF16 = jnp.bfloat16
F32 = jnp.float32
MAX_COPIES = 192
MAX_LOCAL = 64


def kernel(
    lin, t, out, zl, yl, ag, mt, g, ob, rz, rx, s0, s1, f0, f1, fo, mo, ssem, rsem, lsem
):
    r = lax.axis_index("row")
    col = lax.axis_index("col")
    y, k = lax.div(r, 2), lax.rem(r, 2)
    z, x = lax.div(col, 4), lax.rem(col, 4)

    def around(v):
        return lax.rem(v + 1, 4), lax.rem(v + 3, 4), lax.rem(v + 2, 4)

    xp, xm, x2 = around(x)
    yp, ym, y2 = around(y)
    zp, zm, z2 = around(z)

    def dev(x_=x, y_=y, z_=z, k_=k):
        return (2 * y_ + k_, 4 * z_ + x_)

    count = [0, 0]
    sent = []
    local = []

    def send(src, dst, to):
        i = count[0]
        count[0] += 1
        cp = pltpu.make_async_remote_copy(
            src_ref=src,
            dst_ref=dst,
            send_sem=ssem.at[i],
            recv_sem=rsem.at[i],
            device_id=to,
            device_id_type=MESH,
        )
        cp.start()
        sent.append(cp)
        return cp

    def copy(src, dst):
        i = count[1]
        count[1] += 1
        cp = pltpu.make_async_copy(src, dst, lsem.at[i])
        cp.start()
        return cp

    def exchange(src, dst):
        plans = []
        n = count[0]
        m = count[1]
        count[0] += 2
        count[1] += 2
        slot = lax.rem(x, 2)
        for i in range(2):
            x_to = 2 * k + i
            same = (y == z) & (x == x_to)
            to = dev(x_=x_to, y_=z, z_=y, k_=lax.div(x, 2))

            def remote(lands, i=i, to=to):
                return pltpu.make_async_remote_copy(
                    src_ref=src(i),
                    dst_ref=dst(lands),
                    send_sem=ssem.at[n + i],
                    recv_sem=rsem.at[n + lands],
                    device_id=to,
                    device_id_type=MESH,
                )

            here = pltpu.make_async_copy(src(i), dst(i), lsem.at[m + i])
            plans.append((same, remote(slot), remote(i), here))
        for same, there, back, here in plans:
            pl.when(jnp.logical_not(same))(there.start)
            pl.when(same)(here.start)
        return plans

    def exchange_wait(plans, i):
        same, there, back, here = plans[i]

        def both():
            there.wait_send()
            back.wait_recv()

        pl.when(jnp.logical_not(same))(both)
        pl.when(same)(here.wait)

    mine = copy(lin.at[:, pl.ds(2 * x, 2)], zl.at[z, :, x, pl.ds(0, 2)])
    mine_h = copy(lin.at[:, 8 + lax.div(x, 2)], zl.at[z, :, x, 2])
    mirrored = exchange(lambda i: t.at[i, pl.ds(1, 3)], lambda i: mt.at[i])
    spread = {}
    for off in (1, 3, 2):
        xt = lax.rem(x + off, 4)
        spread[off] = (
            send(lin.at[:, pl.ds(2 * xt, 2)], zl.at[z, :, x, pl.ds(0, 2)], dev(x_=xt)),
            send(lin.at[:, 8 + lax.div(xt, 2)], zl.at[z, :, x, 2], dev(x_=xt)),
        )
    mine.wait()
    mine_h.wait()

    chunk = [x, xm, xp, x2]
    offs = [0, 1, 3, 2]
    zc, yc = {}, {}
    rr = [r, 2 * ym + k, 2 * yp + k, 2 * y2 + k]
    partner = dev(k_=1 - k)
    locals_ = []

    def send_chunk(j):
        xs = chunk[j]
        src = zl.at[z, :, xs]
        zc[j] = [send(src, src, dev(z_=zp)), send(src, src, dev(z_=zm))]
        dst = yl.at[r, :, xs]
        yc[j] = [
            send(src, dst, dev(y_=yp)),
            send(src, dst, dev(y_=ym)),
            send(src, dst, partner),
        ]
        locals_.append(copy(src, dst))

    def forward_chunk(j):
        xs = chunk[j]
        zc[j][0].wait_recv()
        blk = zl.at[zm, 0, xs]
        zc[j].append(send(blk, blk, dev(z_=zp)))
        zc[j][1].wait_recv()
        blk = zl.at[zp, 1, xs]
        zc[j].append(send(blk, blk, dev(z_=zm)))
        yc[j][0].wait_recv()
        blk = yl.at[rr[1], 0, xs]
        yc[j].append(send(blk, blk, dev(y_=yp)))
        blk = yl.at[rr[1], :, xs]
        yc[j].append(send(blk, blk, partner))
        yc[j][1].wait_recv()
        blk = yl.at[rr[2], 1, xs]
        yc[j].append(send(blk, blk, dev(y_=ym)))
        blk = yl.at[rr[2], :, xs]
        yc[j].append(send(blk, blk, partner))

    def finish_chunk(j):
        xs = chunk[j]
        yc[j][3].wait_recv()
        yc[j][5].wait_recv()
        blk = yl.at[rr[3], :, xs]
        yc[j].append(send(blk, blk, partner))

    ac, pc = {}, []

    def send_a(b):
        blk = ag.at[rr[b], :, x]
        ac[b] = [
            send(blk, blk, dev(x_=xp)),
            send(blk, blk, dev(x_=xm)),
        ]
        pc.append(send(blk, blk, partner))

    def forward_a(b):
        ac[b][0].wait_recv()
        blk = ag.at[rr[b], 0, xm]
        ac[b].append(send(blk, blk, dev(x_=xp)))
        blk = ag.at[rr[b], :, xm]
        pc.append(send(blk, blk, partner))
        ac[b][1].wait_recv()
        blk = ag.at[rr[b], 1, xp]
        ac[b].append(send(blk, blk, dev(x_=xm)))
        blk = ag.at[rr[b], :, xp]
        pc.append(send(blk, blk, partner))

    def finish_a(b):
        ac[b][2].wait_recv()
        ac[b][3].wait_recv()
        blk = ag.at[rr[b], :, x2]
        pc.append(send(blk, blk, partner))

    send_chunk(0)

    for i in range(2):
        exchange_wait(mirrored, i)
    for i in range(2):
        for p, (own, other) in enumerate(((0, 1), (1, 0), (3, 2))):
            diff = t[i, own].astype(F32) - mt[i, other].astype(F32).T
            ag[r, i, x, p] = diff.astype(BF16)
    blk = ag.at[r, :, x]
    a_up = send(blk, blk, dev(y_=yp))
    a_dn = send(blk, blk, dev(y_=ym))
    send_a(0)

    def arrive(j):
        for cp in spread[offs[j]]:
            cp.wait_recv()
        send_chunk(j)

    arrive(1)
    arrive(2)
    forward_chunk(0)
    a_up.wait_recv()
    blk = ag.at[rr[1], 0, x]
    a_up2 = send(blk, blk, dev(y_=yp))
    send_a(1)
    a_dn.wait_recv()
    blk = ag.at[rr[2], 1, x]
    a_dn2 = send(blk, blk, dev(y_=ym))
    send_a(2)
    arrive(3)
    forward_chunk(1)
    forward_a(0)
    forward_chunk(2)
    a_up2.wait_recv()
    a_dn2.wait_recv()
    send_a(3)
    forward_a(1)
    forward_a(2)
    forward_chunk(3)
    forward_a(3)
    for j in range(4):
        finish_chunk(j)
    for b in range(4):
        finish_a(b)
    for j in range(4):
        zc[j][2].wait_recv()
        zc[j][3].wait_recv()
        for n in (2, 4, 6, 7):
            yc[j][n].wait_recv()
    for cp in pc:
        cp.wait_recv()
    for cp in locals_:
        cp.wait()

    half = 2 * lax.rem(x, 2)
    red = {}

    def lhs_of(q):
        rows = [
            jnp.concatenate(
                [zl[dz, i, dx, q] for dz in range(4) for dx in range(4)], axis=1
            )
            for i in range(2)
        ]
        return jnp.concatenate(rows, axis=0)

    for p in range(3):
        full = jnp.concatenate(
            [
                jnp.concatenate([ag[d // 2, d % 2, c, p] for c in range(4)], axis=1)
                for d in range(16)
            ],
            axis=0,
        )
        for q in range(2):
            g[p, :, q * 512 : (q + 1) * 512] = jnp.dot(
                lhs_of(q), full, preferred_element_type=F32
            ).astype(BF16)
        part = jnp.concatenate(
            [
                jnp.concatenate(
                    [ag[d // 2, d % 2, half + c, p] for c in range(2)], axis=1
                )
                for d in range(16)
            ],
            axis=0,
        )
        g[p, :, 1024:1280] = jnp.dot(
            lhs_of(2), part, preferred_element_type=F32
        ).astype(BF16)

        def tile_pair(a, carry, p=p):
            rows = []
            for i in range(2):
                tiles = [yl[a, i, c, q] for q in range(2) for c in range(4)]
                tiles += [yl[a, i, half + c, 2] for c in range(2)]
                rows.append(jnp.concatenate(tiles, axis=1))
            right = jnp.concatenate(rows, axis=0)
            res = lax.dot_general(
                g[p],
                right,
                (((1,), (1,)), ((), ())),
                preferred_element_type=F32,
            ).astype(BF16)
            az, ax = lax.div(a, 2), 2 * lax.rem(a, 2)
            for i in range(2):
                for n in range(2):
                    ob[p, i, az, ax + n] = res[
                        i * 128 : (i + 1) * 128, n * 128 : (n + 1) * 128
                    ]
            return carry

        lax.fori_loop(0, 8, tile_pair, 0)
        red[p] = []
        for off in (1, 3, 2):
            zt, xt = lax.rem(z + off, 4), lax.rem(x + off, 4)
            red[p].append(send(ob.at[p, 0, zt], rz.at[p, z], dev(z_=zt)))
            red[p].append(send(ob.at[p, 1, :, xt], rx.at[p, x], dev(x_=xt)))
        rz[p, z] = ob[p, 0, z]
        rx[p, x] = ob[p, 1, :, x]

    last = {}

    def total(ref, p):
        acc = ref[p, 0].astype(F32)
        for n in range(1, 4):
            acc = acc + ref[p, n].astype(F32)
        return acc.astype(BF16)

    for p in range(3):
        for cp in red[p]:
            cp.wait_recv()
        s0[p] = total(rz, p)
        s1[p] = total(rx, p)
        last[p] = []
        for off in (1, 3, 2):
            zt, xt = lax.rem(z + off, 4), lax.rem(x + off, 4)
            last[p].append(send(s0.at[p, xt], f0.at[p, x], dev(x_=xt)))
            last[p].append(send(s1.at[p, zt], f1.at[p, z], dev(z_=zt)))
        f0[p, x] = s0[p, x]
        f1[p, z] = s1[p, z]

    for p in range(3):
        for cp in last[p]:
            cp.wait_recv()
        to = (1, 0, 3)[p]
        tiles = (total(f0, p), total(f1, p))
        for i in range(2):
            out[i, 0, to] = tiles[i]
            if p == 0:
                fo[i] = tiles[i]
        if p == 0:
            swapped = exchange(lambda i: fo.at[i], lambda i: mo.at[i])
    for i in range(2):
        exchange_wait(swapped, i)
    for i in range(2):
        out[i, 0, 2] = (-mo[i].astype(F32).T).astype(BF16)
    for cp in sent:
        cp.wait_send()


def body(amplitudes, cholesky, tile_mask):
    keep = (tile_mask != 0)[:, :, None, None]
    amp = amplitudes[:, 0]
    order = jnp.stack([amp[:, p] for p in (1, 0, 2, 3)], axis=1)
    masked = jnp.where(keep, order, jnp.zeros_like(order))
    vec = cholesky[:, 0]
    vmem = pl.BlockSpec(memory_space=pltpu.VMEM)
    tile = (128, 128)
    return pl.pallas_call(
        kernel,
        out_shape=jax.ShapeDtypeStruct((2, 1, 4) + tile, BF16),
        in_specs=[vmem, vmem],
        out_specs=vmem,
        scratch_shapes=[
            pltpu.VMEM((4, 2, 4, 3) + tile, BF16),
            pltpu.VMEM((8, 2, 4, 3) + tile, BF16),
            pltpu.VMEM((8, 2, 4, 3) + tile, BF16),
            pltpu.VMEM((2, 3) + tile, BF16),
            pltpu.VMEM((3, 256, 1280), BF16),
            pltpu.VMEM((3, 2, 4, 4) + tile, BF16),
            pltpu.VMEM((3, 4, 4) + tile, BF16),
            pltpu.VMEM((3, 4, 4) + tile, BF16),
            pltpu.VMEM((3, 4) + tile, BF16),
            pltpu.VMEM((3, 4) + tile, BF16),
            pltpu.VMEM((3, 4) + tile, BF16),
            pltpu.VMEM((3, 4) + tile, BF16),
            pltpu.VMEM((2,) + tile, BF16),
            pltpu.VMEM((2,) + tile, BF16),
            pltpu.SemaphoreType.DMA((MAX_COPIES,)),
            pltpu.SemaphoreType.DMA((MAX_COPIES,)),
            pltpu.SemaphoreType.DMA((MAX_LOCAL,)),
        ],
        compiler_params=pltpu.CompilerParams(
            has_side_effects=True, vmem_limit_bytes=56 * 1024 * 1024
        ),
    )(vec, masked)


def solution(mesh):
    in_specs = (
        P("row", "col", None, None, None),
        P("row", "col", None, None, None),
        P("row", "col"),
    )
    out_specs = P("row", "col", None, None, None)
    return jax.shard_map(
        body, mesh=mesh, in_specs=in_specs, out_specs=out_specs, check_vma=False
    )
```

```python
import math

import jax
import jax.numpy as jnp
from jax import lax
from jax.experimental import pallas as pl
from jax.experimental.pallas import tpu as pltpu
from jax.sharding import PartitionSpec as P

MESH = pl.DeviceIdType.MESH
BF16 = jnp.bfloat16
F32 = jnp.float32
SENDS = 6
RECVS = 110
LOCALS = 16


def kernel(
    mask, lin, t_in, out, t, zl, yl, ag, mt, g, ob, rz, rx, s0, s1, f0, f1, fo, mo,
    size, ssem, rsem, lsem, xsem,
):
    r = lax.axis_index("row")
    col = lax.axis_index("col")
    y, k = lax.div(r, 2), lax.rem(r, 2)
    z, x = lax.div(col, 4), lax.rem(col, 4)

    def ring(v):
        return v, lax.rem(v + 3, 4), lax.rem(v + 1, 4), lax.rem(v + 2, 4)

    xs, ys, zs = ring(x), ring(y), ring(z)

    def dev(x_=x, y_=y, z_=z, k_=k):
        return (2 * y_ + k_, 4 * z_ + x_)

    to_x = [dev(x_=v) for v in xs]
    to_y = [dev(y_=v) for v in ys]
    to_z = [dev(z_=v) for v in zs]
    partner = dev(k_=1 - k)

    used = {"recv": 0, "local": 0, "swap": 0}
    load = [0] * SENDS

    def arrival():
        used["recv"] += 1
        return [rsem.at[used["recv"] - 1], 0]

    def await_tiles(due):
        blk = size.at[pl.ds(0, due[1])]
        pltpu.make_async_copy(blk, blk, due[0]).wait()

    def send(src, dst, to, group, due=None):
        due = due or arrival()
        tiles = math.prod(src.shape) // (128 * 128)
        due[1] += tiles
        load[group] += tiles
        pltpu.make_async_remote_copy(
            src_ref=src,
            dst_ref=dst,
            send_sem=ssem.at[group],
            recv_sem=due[0],
            device_id=to,
            device_id_type=MESH,
        ).start()
        return due

    def copy(src, dst):
        cp = pltpu.make_async_copy(src, dst, lsem.at[used["local"]])
        used["local"] += 1
        cp.start()
        return cp

    def mirror_of(i):
        return (y == z) & (x == 2 * k + i), dev(
            x_=2 * k + i, y_=z, z_=y, k_=lax.div(x, 2)
        )

    def exchange(src, dst):
        plans = []
        n = used["swap"]
        used["swap"] += 6
        slot = lax.rem(x, 2)
        for i in range(2):
            same, to = mirror_of(i)

            def remote(lands, i=i, to=to):
                return pltpu.make_async_remote_copy(
                    src_ref=src(i),
                    dst_ref=dst(lands),
                    send_sem=xsem.at[n + i],
                    recv_sem=xsem.at[n + 2 + lands],
                    device_id=to,
                    device_id_type=MESH,
                )

            here = pltpu.make_async_copy(src(i), dst(i), xsem.at[n + 4 + i])
            plans.append((same, remote(slot), remote(i), here))
        for same, there, back, here in plans:
            pl.when(jnp.logical_not(same))(there.start)
            pl.when(same)(here.start)
        return plans

    def exchange_wait(plans):
        for same, there, back, here in plans:

            def both(there=there, back=back):
                there.wait_send()
                back.wait_recv()

            pl.when(jnp.logical_not(same))(both)
            pl.when(same)(here.wait)

    barrier = pltpu.get_barrier_semaphore()

    def greet(to):
        pl.semaphore_signal(barrier, inc=1, device_id=to, device_id_type=MESH)

    selfs = jnp.int32(0)
    for i in range(2):
        same, to = mirror_of(i)
        selfs = selfs + jnp.where(same, 1, 0)
        pl.when(jnp.logical_not(same))(lambda to=to: greet(to))
    near = to_z[1:] + to_x[1:] + to_y[1:3] + [partner]
    for to in near:
        greet(to)
    mine = copy(lin.at[:, pl.ds(2 * x, 2)], zl.at[z, :, x, pl.ds(0, 2)])
    mine_h = copy(lin.at[:, 8 + lax.div(x, 2)], zl.at[z, :, x, 2])
    for i in range(2):
        flag = mask[0, i].astype(F32)
        for p in range(4):
            tile = (t_in[i, 0, p].astype(F32) * flag).astype(BF16)
            if p:
                t[i, p - 1] = tile
            else:
                ag[0, y, k, i, x] = tile
    mine.wait()
    mine_h.wait()
    pl.semaphore_wait(barrier, len(near) + 2 - selfs)

    class Gather:
        def __init__(self, p, y_first):
            self.p = p
            self.y_first = y_first
            self.one, self.two = (to_y, to_x) if y_first else (to_x, to_y)
            self.near = [None] * 4
            self.far = arrival()
            self.other = arrival()

        def block(self, n, m, rows=slice(None)):
            a, b = (n, m) if self.y_first else (m, n)
            return ag.at[self.p, ys[a], k, rows, xs[b]]

        def spread_second(self, n):
            blk = self.block(n, 0)
            self.near[n] = [
                send(blk, blk, self.two[2], 3),
                send(blk, blk, self.two[1], 3),
            ]

        def start(self):
            blk = self.block(0, 0)
            self.first = [send(blk, blk, self.one[2], 3), send(blk, blk, self.one[1], 3)]
            self.first.append(arrival())

        def middle(self):
            for n, row, m in ((1, 0, 2), (2, 1, 1)):
                await_tiles(self.first[n - 1])
                blk = self.block(n, 0, row)
                send(blk, blk, self.one[m], 3, self.first[2])
                self.spread_second(n)

        def across(self):
            await_tiles(self.first[2])
            self.spread_second(3)
            self.hand_over(0)

        def forward(self, n):
            for b, row, m in ((1, 0, 2), (2, 1, 1)):
                await_tiles(self.near[n][b - 1])
                blk = self.block(n, b, row)
                send(blk, blk, self.two[m], 3, self.far)

        def hand_over(self, m):
            if self.y_first:
                blk = ag.at[self.p, :, k, :, xs[m]]
            else:
                blk = ag.at[self.p, ys[m], k]
            send(blk, blk, partner, 4, self.other)

        def hand_near(self):
            self.hand_over(1)
            self.hand_over(2)

        def hand_far(self):
            await_tiles(self.far)
            self.hand_over(3)

        def done(self):
            await_tiles(self.other)

    a0, a1, a2 = (Gather(p, True) for p in range(3))

    a0.start()
    swaps = [
        exchange(lambda i, q=q: t.at[i, q], lambda i, q=q: mt.at[q - 1, i])
        for q in (1, 2)
    ]

    def form(p):
        own, other = ((0, 0), (2, 1))[p - 1]
        exchange_wait(swaps[p - 1])
        for i in range(2):
            diff = t[i, own].astype(F32) - mt[other, i].astype(F32).T
            ag[p, y, k, i, x] = diff.astype(BF16)

    spread = [None] * 4
    for n, m in ((1, 2), (2, 1), (3, 3)):
        v = xs[m]
        spread[n] = arrival()
        src = lin.at[:, pl.ds(2 * v, 2)]
        send(src, zl.at[z, :, x, pl.ds(0, 2)], to_x[m], 0, spread[n])
        src = lin.at[:, 8 + lax.div(v, 2)]
        send(src, zl.at[z, :, x, 2], to_x[m], 0, spread[n])

    zc, yc, yp = [None] * 4, [None] * 4, [None] * 4
    depth = (3, 2, 2, 3)
    own_copies = []

    def z_send(j):
        src = zl.at[z, :, xs[j]]
        zc[j] = [send(src, src, to_z[2], 0), send(src, src, to_z[1], 0), arrival()]

    def z_forward(j):
        for n, row, m in ((1, 0, 2), (2, 1, 1)):
            await_tiles(zc[j][n - 1])
            blk = zl.at[zs[n], row, xs[j]]
            send(blk, blk, to_z[m], 0, zc[j][2])

    def y_block(j, n, rows=slice(None)):
        return yl.at[ys[n], k, rows, xs[j], pl.ds(0, depth[j])]

    def y_send(j):
        src = zl.at[z, :, xs[j], pl.ds(0, depth[j])]
        dst = y_block(j, 0)
        yc[j] = [send(src, dst, to_y[2], 1), send(src, dst, to_y[1], 1), arrival()]
        yp[j] = send(src, dst, partner, 2)
        own_copies.append(copy(src, dst))

    def y_forward(j):
        for n, row, m in ((1, 0, 2), (2, 1, 1)):
            await_tiles(yc[j][n - 1])
            blk = y_block(j, n, row)
            send(blk, blk, to_y[m], 1, yc[j][2])
            blk = y_block(j, n)
            send(blk, blk, partner, 2, yp[j])

    def y_finish(j):
        await_tiles(yc[j][2])
        blk = y_block(j, 3)
        send(blk, blk, partner, 2, yp[j])

    half = lax.rem(x, 2)
    red, last = {}, {}

    def lhs_of(q):
        rows = [
            jnp.concatenate(
                [zl[dz, i, dx, q] for dz in range(4) for dx in range(4)], axis=1
            )
            for i in range(2)
        ]
        return jnp.concatenate(rows, axis=0)

    def rhs_of(p, columns):
        rows = [
            jnp.concatenate(
                [ag[p, d // 4, d % 4 // 2, d % 2, c] for c in columns], axis=1
            )
            for d in range(16)
        ]
        return jnp.concatenate(rows, axis=0)

    def first_half(p, q):
        if q < 2:
            g[p, :, q * 512 : (q + 1) * 512] = jnp.dot(
                lhs_of(q), rhs_of(p, range(4)), preferred_element_type=F32
            ).astype(BF16)
        else:
            g[p, :, 1024:1280] = jnp.dot(
                lhs_of(2), rhs_of(p, (half, half + 2)), preferred_element_type=F32
            ).astype(BF16)

    def second_half(p, n):
        ay = zs[n]

        def tile_pair(ak, carry):
            rows = []
            for i in range(2):
                tiles = [yl[ay, ak, i, c, q] for q in range(2) for c in range(4)]
                tiles += [yl[ay, ak, i, half + 2 * c, 2] for c in range(2)]
                rows.append(jnp.concatenate(tiles, axis=1))
            right = jnp.concatenate(rows, axis=0)
            res = lax.dot_general(
                g[p],
                right,
                (((1,), (1,)), ((), ())),
                preferred_element_type=F32,
            ).astype(BF16)
            for i in range(2):
                for n in range(2):
                    ob[p, i, ay, 2 * ak + n] = res[
                        i * 128 : (i + 1) * 128, n * 128 : (n + 1) * 128
                    ]
            return carry

        lax.fori_loop(0, 2, tile_pair, 0)
        if p not in red:
            red[p] = [arrival(), arrival()]
        if n:
            send(ob.at[p, 0, ay], rz.at[p, z], to_z[n], 5, red[p][0])
        for m in (3, 1, 2):
            src = ob.at[p, 1, ay, xs[m]]
            send(src, rx.at[p, x, ay], to_x[m], 5, red[p][1])
        if not n:
            rz[p, z] = ob[p, 0, z]
            rx[p, x] = ob[p, 1, :, x]

    def total(ref, p):
        acc = ref[p, 0].astype(F32)
        for n in range(1, 4):
            acc = acc + ref[p, n].astype(F32)
        return acc.astype(BF16)

    def reduce_first(p):
        last[p] = [arrival(), arrival()]
        await_tiles(red[p][0])
        s0[p] = total(rz, p)
        for n in (3, 1, 2):
            send(s0.at[p, xs[n]], f0.at[p, x], to_x[n], 5, last[p][0])
        f0[p, x] = s0[p, x]
        await_tiles(red[p][1])
        s1[p] = total(rx, p)
        for n in (3, 1, 2):
            send(s1.at[p, zs[n]], f1.at[p, z], to_z[n], 5, last[p][1])
        f1[p, z] = s1[p, z]

    def reduce_last(p):
        for i, ref in enumerate((f0, f1)):
            await_tiles(last[p][i])
            tile = total(ref, p)
            if p:
                out[i, 0, (1, 3)[p - 1]] = tile
            if p < 2:
                fo[p, i] = tile

    z_send(0)
    y_send(0)
    a0.spread_second(0)
    a0.middle()
    a0.across()
    y_forward(0)
    z_forward(0)
    await_tiles(spread[1])
    z_send(1)
    y_send(1)
    await_tiles(spread[2])
    z_send(2)
    y_send(2)
    await_tiles(spread[3])
    z_send(3)
    a0.forward(0)
    form(1)
    a1.start()
    a1.spread_second(0)
    form(2)
    a2.start()
    y_send(3)
    a0.forward(1)
    a0.forward(2)
    y_forward(1)
    z_forward(1)
    a1.middle()
    a2.spread_second(0)
    a2.middle()
    y_forward(2)
    a0.forward(3)
    a1.across()
    a2.across()
    z_forward(2)
    a0.hand_near()
    y_finish(0)
    y_finish(1)
    a0.hand_far()
    z_forward(3)
    y_forward(3)
    y_finish(2)
    a1.forward(0)
    a1.forward(1)
    a1.forward(2)
    a1.forward(3)
    a1.hand_near()
    a2.forward(0)
    for j in range(4):
        await_tiles(zc[j][2])
    a0.done()
    first_half(0, 0)
    y_finish(3)
    a2.forward(1)
    a2.forward(2)
    first_half(0, 1)
    a1.hand_far()
    a2.forward(3)
    a2.hand_near()
    first_half(0, 2)
    for j in range(4):
        await_tiles(yp[j])
    for cp in own_copies:
        cp.wait()
    second_half(0, 3)
    second_half(0, 1)
    a2.hand_far()
    second_half(0, 2)
    second_half(0, 0)
    a1.done()
    for q in range(3):
        first_half(1, q)
    for n in (3, 1, 2, 0):
        second_half(1, n)
    reduce_first(0)
    a2.done()
    for q in range(3):
        first_half(2, q)
    reduce_last(0)
    back0 = exchange(lambda i: fo.at[0, i], lambda i: mo.at[0, i])
    second_half(2, 3)
    second_half(2, 1)
    reduce_first(1)
    second_half(2, 2)
    second_half(2, 0)
    reduce_last(1)
    back1 = exchange(lambda i: fo.at[1, i], lambda i: mo.at[1, i])
    exchange_wait(back0)
    for i in range(2):
        diff = fo[0, i].astype(F32) - mo[0, i].astype(F32).T
        out[i, 0, 0] = diff.astype(BF16)
    reduce_first(2)
    exchange_wait(back1)
    for i in range(2):
        out[i, 0, 2] = (-mo[1, i].astype(F32).T).astype(BF16)
    reduce_last(2)
    for n in range(SENDS):
        await_tiles([ssem.at[n], load[n]])


def body(amplitudes, cholesky, tile_mask):
    vec = cholesky[:, 0]
    vmem = pl.BlockSpec(memory_space=pltpu.VMEM)
    tile = (128, 128)
    return pl.pallas_call(
        kernel,
        out_shape=jax.ShapeDtypeStruct((2, 1, 4) + tile, BF16),
        in_specs=[pl.BlockSpec(memory_space=pltpu.SMEM), vmem, vmem],
        out_specs=vmem,
        scratch_shapes=[
            pltpu.VMEM((2, 3) + tile, BF16),
            pltpu.VMEM((4, 2, 4, 3) + tile, BF16),
            pltpu.VMEM((4, 2, 2, 4, 3) + tile, BF16),
            pltpu.VMEM((3, 4, 2, 2, 4) + tile, BF16),
            pltpu.VMEM((2, 2) + tile, BF16),
            pltpu.VMEM((3, 256, 1280), BF16),
            pltpu.VMEM((3, 2, 4, 4) + tile, BF16),
            pltpu.VMEM((3, 4, 4) + tile, BF16),
            pltpu.VMEM((3, 4, 4) + tile, BF16),
            pltpu.VMEM((3, 4) + tile, BF16),
            pltpu.VMEM((3, 4) + tile, BF16),
            pltpu.VMEM((3, 4) + tile, BF16),
            pltpu.VMEM((3, 4) + tile, BF16),
            pltpu.VMEM((2, 2) + tile, BF16),
            pltpu.VMEM((2, 2) + tile, BF16),
            pltpu.VMEM((256,) + tile, BF16),
            pltpu.SemaphoreType.DMA((SENDS,)),
            pltpu.SemaphoreType.DMA((RECVS,)),
            pltpu.SemaphoreType.DMA((LOCALS,)),
            pltpu.SemaphoreType.DMA((24,)),
        ],
        compiler_params=pltpu.CompilerParams(
            collective_id=0, has_side_effects=True, vmem_limit_bytes=56 * 1024 * 1024
        ),
    )(tile_mask.T, vec, amplitudes)


def solution(mesh):
    in_specs = (
        P("row", "col", None, None, None),
        P("row", "col", None, None, None),
        P("row", "col"),
    )
    out_specs = P("row", "col", None, None, None)
    return jax.shard_map(
        body, mesh=mesh, in_specs=in_specs, out_specs=out_specs, check_vma=False
    )
```

```python
import math

import jax
import jax.numpy as jnp
from jax import lax
from jax.experimental import pallas as pl
from jax.experimental.pallas import tpu as pltpu
from jax.sharding import PartitionSpec as P

MESH = pl.DeviceIdType.MESH
BF16 = jnp.bfloat16
F32 = jnp.float32
SENDS = 6
RECVS = 110
LOCALS = 16


def kernel(
    mask, lin, t_in, out, t, zl, yl, ag, mt, g, ob, rz, rx, s0, s1, f0, f1, fo, mo,
    qz, qx, cz, cx, size, ssem, rsem, lsem, xsem,
):
    r = lax.axis_index("row")
    col = lax.axis_index("col")
    y, k = lax.div(r, 2), lax.rem(r, 2)
    z, x = lax.div(col, 4), lax.rem(col, 4)

    def ring(v):
        return v, lax.rem(v + 3, 4), lax.rem(v + 1, 4), lax.rem(v + 2, 4)

    xs, ys, zs = ring(x), ring(y), ring(z)

    def dev(x_=x, y_=y, z_=z, k_=k):
        return (2 * y_ + k_, 4 * z_ + x_)

    to_x = [dev(x_=v) for v in xs]
    to_y = [dev(y_=v) for v in ys]
    to_z = [dev(z_=v) for v in zs]
    partner = dev(k_=1 - k)

    used = {"recv": 0, "local": 0, "swap": 0}
    load = [0] * SENDS

    def arrival():
        used["recv"] += 1
        return [rsem.at[used["recv"] - 1], 0]

    def await_tiles(due):
        blk = size.at[pl.ds(0, due[1])]
        pltpu.make_async_copy(blk, blk, due[0]).wait()

    def send(src, dst, to, group, due=None):
        due = due or arrival()
        tiles = math.prod(src.shape) // (128 * 128)
        due[1] += tiles
        load[group] += tiles
        pltpu.make_async_remote_copy(
            src_ref=src,
            dst_ref=dst,
            send_sem=ssem.at[group],
            recv_sem=due[0],
            device_id=to,
            device_id_type=MESH,
        ).start()
        return due

    def copy(src, dst):
        cp = pltpu.make_async_copy(src, dst, lsem.at[used["local"]])
        used["local"] += 1
        cp.start()
        return cp

    def mirror_of(i):
        return (y == z) & (x == 2 * k + i), dev(
            x_=2 * k + i, y_=z, z_=y, k_=lax.div(x, 2)
        )

    def exchange(src, dst):
        plans = []
        n = used["swap"]
        used["swap"] += 6
        slot = lax.rem(x, 2)
        for i in range(2):
            same, to = mirror_of(i)

            def remote(lands, i=i, to=to):
                return pltpu.make_async_remote_copy(
                    src_ref=src(i),
                    dst_ref=dst(lands),
                    send_sem=xsem.at[n + i],
                    recv_sem=xsem.at[n + 2 + lands],
                    device_id=to,
                    device_id_type=MESH,
                )

            here = pltpu.make_async_copy(src(i), dst(i), xsem.at[n + 4 + i])
            plans.append((same, remote(slot), remote(i), here))
        for same, there, back, here in plans:
            pl.when(jnp.logical_not(same))(there.start)
            pl.when(same)(here.start)
        return plans

    def exchange_wait(plans):
        for same, there, back, here in plans:

            def both(there=there, back=back):
                there.wait_send()
                back.wait_recv()

            pl.when(jnp.logical_not(same))(both)
            pl.when(same)(here.wait)

    barrier = pltpu.get_barrier_semaphore()

    def greet(to):
        pl.semaphore_signal(barrier, inc=1, device_id=to, device_id_type=MESH)

    selfs = jnp.int32(0)
    for i in range(2):
        same, to = mirror_of(i)
        selfs = selfs + jnp.where(same, 1, 0)
        pl.when(jnp.logical_not(same))(lambda to=to: greet(to))
    near = to_z[1:] + to_x[1:] + to_y[1:3] + [partner]
    for to in near:
        greet(to)
    mine = copy(lin.at[:, pl.ds(2 * x, 2)], zl.at[z, :, x, pl.ds(0, 2)])
    mine_h = copy(lin.at[:, 8 + lax.div(x, 2)], zl.at[z, :, x, 2])
    for i in range(2):
        flag = mask[0, i].astype(F32)
        for p in range(4):
            tile = (t_in[i, 0, p].astype(F32) * flag).astype(BF16)
            if p:
                t[i, p - 1] = tile
            else:
                ag[0, y, k, i, x] = tile
    mine.wait()
    mine_h.wait()
    pl.semaphore_wait(barrier, len(near) + 2 - selfs)

    class Gather:
        def __init__(self, p, y_first):
            self.p = p
            self.y_first = y_first
            self.one, self.two = (to_y, to_x) if y_first else (to_x, to_y)
            self.near = [None] * 4
            self.far = arrival()
            self.other = arrival()

        def block(self, n, m, rows=slice(None)):
            a, b = (n, m) if self.y_first else (m, n)
            return ag.at[self.p, ys[a], k, rows, xs[b]]

        def spread_second(self, n):
            blk = self.block(n, 0)
            self.near[n] = [
                send(blk, blk, self.two[2], 3),
                send(blk, blk, self.two[1], 3),
            ]

        def start(self):
            blk = self.block(0, 0)
            self.first = [send(blk, blk, self.one[2], 3), send(blk, blk, self.one[1], 3)]
            self.first.append(arrival())

        def middle(self):
            for n, row, m in ((1, 0, 2), (2, 1, 1)):
                await_tiles(self.first[n - 1])
                blk = self.block(n, 0, row)
                send(blk, blk, self.one[m], 3, self.first[2])
                self.spread_second(n)

        def across(self):
            await_tiles(self.first[2])
            self.spread_second(3)
            self.hand_over(0)

        def forward(self, n):
            for b, row, m in ((1, 0, 2), (2, 1, 1)):
                await_tiles(self.near[n][b - 1])
                blk = self.block(n, b, row)
                send(blk, blk, self.two[m], 3, self.far)

        def hand_over(self, m):
            if self.y_first:
                blk = ag.at[self.p, :, k, :, xs[m]]
            else:
                blk = ag.at[self.p, ys[m], k]
            send(blk, blk, partner, 4, self.other)

        def hand_near(self):
            self.hand_over(1)
            self.hand_over(2)

        def hand_far(self):
            await_tiles(self.far)
            self.hand_over(3)

        def done(self):
            await_tiles(self.other)

    a0, a1, a2 = (Gather(p, True) for p in range(3))

    a0.start()
    def swap(q):
        swaps.append(exchange(lambda i: t.at[i, q], lambda i: mt.at[q - 1, i]))

    swaps = []
    swap(1)

    def form(p):
        own, other = ((0, 0), (2, 1))[p - 1]
        exchange_wait(swaps[p - 1])
        for i in range(2):
            diff = t[i, own].astype(F32) - mt[other, i].astype(F32).T
            ag[p, y, k, i, x] = diff.astype(BF16)

    spread = [None] * 4
    for n, m in ((1, 2), (2, 1), (3, 3)):
        v = xs[m]
        spread[n] = arrival()
        src = lin.at[:, pl.ds(2 * v, 2)]
        send(src, zl.at[z, :, x, pl.ds(0, 2)], to_x[m], 0, spread[n])
        src = lin.at[:, 8 + lax.div(v, 2)]
        send(src, zl.at[z, :, x, 2], to_x[m], 0, spread[n])

    zc, yc, yp = [None] * 4, [None] * 4, [None] * 4
    depth = (3, 2, 2, 3)
    own_copies = []

    def z_send(j):
        src = zl.at[z, :, xs[j]]
        zc[j] = [send(src, src, to_z[2], 0), send(src, src, to_z[1], 0), arrival()]

    def z_forward(j):
        for n, row, m in ((1, 0, 2), (2, 1, 1)):
            await_tiles(zc[j][n - 1])
            blk = zl.at[zs[n], row, xs[j]]
            send(blk, blk, to_z[m], 0, zc[j][2])

    def y_block(j, n, rows=slice(None)):
        return yl.at[ys[n], k, rows, xs[j], pl.ds(0, depth[j])]

    def y_send(j):
        src = zl.at[z, :, xs[j], pl.ds(0, depth[j])]
        dst = y_block(j, 0)
        yc[j] = [send(src, dst, to_y[2], 1), send(src, dst, to_y[1], 1), arrival()]
        yp[j] = send(src, dst, partner, 2)
        own_copies.append(copy(src, dst))

    def y_forward(j):
        for n, row, m in ((1, 0, 2), (2, 1, 1)):
            await_tiles(yc[j][n - 1])
            blk = y_block(j, n, row)
            send(blk, blk, to_y[m], 1, yc[j][2])
            blk = y_block(j, n)
            send(blk, blk, partner, 2, yp[j])

    def y_finish(j):
        await_tiles(yc[j][2])
        blk = y_block(j, 3)
        send(blk, blk, partner, 2, yp[j])

    half = lax.rem(x, 2)
    red, relay, last = {}, {}, {}

    def lhs_of(q):
        rows = [
            jnp.concatenate(
                [zl[dz, i, dx, q] for dz in range(4) for dx in range(4)], axis=1
            )
            for i in range(2)
        ]
        return jnp.concatenate(rows, axis=0)

    def rhs_of(p, columns):
        rows = [
            jnp.concatenate(
                [ag[p, d // 4, d % 4 // 2, d % 2, c] for c in columns], axis=1
            )
            for d in range(16)
        ]
        return jnp.concatenate(rows, axis=0)

    def first_half(p, q):
        if q < 2:
            g[p, :, q * 512 : (q + 1) * 512] = jnp.dot(
                lhs_of(q), rhs_of(p, range(4)), preferred_element_type=F32
            ).astype(BF16)
        else:
            g[p, :, 1024:1280] = jnp.dot(
                lhs_of(2), rhs_of(p, (half, half + 2)), preferred_element_type=F32
            ).astype(BF16)

    def second_half(p, n):
        ay = zs[n]

        def tile_pair(ak, carry):
            rows = []
            for i in range(2):
                tiles = [yl[ay, ak, i, c, q] for q in range(2) for c in range(4)]
                tiles += [yl[ay, ak, i, half + 2 * c, 2] for c in range(2)]
                rows.append(jnp.concatenate(tiles, axis=1))
            right = jnp.concatenate(rows, axis=0)
            res = lax.dot_general(
                g[p],
                right,
                (((1,), (1,)), ((), ())),
                preferred_element_type=F32,
            ).astype(BF16)
            for i in range(2):
                for n in range(2):
                    ob[p, i, ay, 2 * ak + n] = res[
                        i * 128 : (i + 1) * 128, n * 128 : (n + 1) * 128
                    ]
            return carry

        lax.fori_loop(0, 2, tile_pair, 0)
        if p not in red:
            red[p] = [arrival(), arrival()]
            relay[p] = [arrival(), arrival()]
        lo, hi = pl.ds(0, 2), pl.ds(2, 2)
        row = ob.at[p, 0, ay]
        if n == 3:
            send(row.at[lo], qz.at[p, lo], to_z[2], 5, relay[p][0])
            send(row.at[hi], qz.at[p, hi], to_z[1], 5, relay[p][0])
        elif n == 2:
            send(row.at[hi], rz.at[p, 1, hi], to_z[2], 5, red[p][0])
        elif n == 1:
            send(row.at[lo], rz.at[p, 2, lo], to_z[1], 5, red[p][0])
        else:
            rz[p, 0] = ob[p, 0, z]
        up = n in (3, 1)
        tile = ob.at[p, 1, ay]
        send(tile.at[xs[3]], qx.at[p, ay], to_x[2 if up else 1], 5, relay[p][1])
        if up:
            send(tile.at[xs[1]], rx.at[p, 2, ay], to_x[1], 5, red[p][1])
        else:
            send(tile.at[xs[2]], rx.at[p, 1, ay], to_x[2], 5, red[p][1])
        rx[p, 0, ay] = ob[p, 1, ay, x]

    def reduce_relayed(p):
        await_tiles(relay[p][0])
        for n, m, part in ((2, 1, slice(0, 2)), (1, 2, slice(2, 4))):
            both = ob[p, 0, zs[n], part].astype(F32) + qz[p, part].astype(F32)
            cz[p, part] = both.astype(BF16)
            part = pl.ds(part.start, 2)
            send(cz.at[p, part], rz.at[p, m, part], to_z[n], 5, red[p][0])
        await_tiles(relay[p][1])
        for n in (3, 1, 2, 0):
            b, m = (2, 1) if n in (3, 1) else (1, 2)
            at = zs[n]
            both = ob[p, 1, at, xs[b]].astype(F32) + qx[p, at].astype(F32)
            cx[p, at] = both.astype(BF16)
            send(cx.at[p, at], rx.at[p, m, at], to_x[b], 5, red[p][1])

    def total(ref, p):
        acc = ref[p, 0].astype(F32)
        for n in range(1, ref.shape[1]):
            acc = acc + ref[p, n].astype(F32)
        return acc.astype(BF16)

    def reduce_first(p):
        last[p] = [arrival(), arrival()]
        await_tiles(red[p][0])
        s0[p] = total(rz, p)
        for n in (3, 1, 2):
            send(s0.at[p, xs[n]], f0.at[p, x], to_x[n], 5, last[p][0])
        f0[p, x] = s0[p, x]
        await_tiles(red[p][1])
        s1[p] = total(rx, p)
        for n in (3, 1, 2):
            send(s1.at[p, zs[n]], f1.at[p, z], to_z[n], 5, last[p][1])
        f1[p, z] = s1[p, z]

    def reduce_last(p):
        for i, ref in enumerate((f0, f1)):
            await_tiles(last[p][i])
            tile = total(ref, p)
            if p:
                out[i, 0, (1, 3)[p - 1]] = tile
            if p < 2:
                fo[p, i] = tile

    z_send(0)
    y_send(0)
    a0.spread_second(0)
    a0.middle()
    swap(2)
    a0.across()
    y_forward(0)
    z_forward(0)
    await_tiles(spread[1])
    z_send(1)
    y_send(1)
    await_tiles(spread[2])
    z_send(2)
    y_send(2)
    await_tiles(spread[3])
    z_send(3)
    a0.forward(0)
    form(1)
    a1.start()
    a1.spread_second(0)
    form(2)
    a2.start()
    y_send(3)
    a0.forward(1)
    a0.forward(2)
    y_forward(1)
    z_forward(1)
    a1.middle()
    a2.spread_second(0)
    a2.middle()
    y_forward(2)
    a0.forward(3)
    a1.across()
    a2.across()
    z_forward(2)
    a0.hand_near()
    y_finish(0)
    y_finish(1)
    a0.hand_far()
    z_forward(3)
    y_forward(3)
    y_finish(2)
    a1.forward(0)
    a1.forward(1)
    a1.forward(2)
    a1.forward(3)
    a1.hand_near()
    a2.forward(0)
    for j in range(4):
        await_tiles(zc[j][2])
    a0.done()
    first_half(0, 0)
    y_finish(3)
    a2.forward(1)
    a2.forward(2)
    first_half(0, 1)
    a1.hand_far()
    a2.forward(3)
    a2.hand_near()
    first_half(0, 2)
    for j in range(4):
        await_tiles(yp[j])
    for cp in own_copies:
        cp.wait()
    second_half(0, 3)
    second_half(0, 1)
    a2.hand_far()
    second_half(0, 2)
    second_half(0, 0)
    a1.done()
    for q in range(3):
        first_half(1, q)
    reduce_relayed(0)
    for n in (3, 1, 2, 0):
        second_half(1, n)
    reduce_first(0)
    a2.done()
    first_half(2, 0)
    first_half(2, 1)
    reduce_relayed(1)
    first_half(2, 2)
    reduce_last(0)
    back0 = exchange(lambda i: fo.at[0, i], lambda i: mo.at[0, i])
    second_half(2, 3)
    second_half(2, 1)
    second_half(2, 2)
    second_half(2, 0)
    reduce_first(1)
    reduce_relayed(2)
    reduce_last(1)
    back1 = exchange(lambda i: fo.at[1, i], lambda i: mo.at[1, i])
    exchange_wait(back0)
    for i in range(2):
        diff = fo[0, i].astype(F32) - mo[0, i].astype(F32).T
        out[i, 0, 0] = diff.astype(BF16)
    reduce_first(2)
    exchange_wait(back1)
    for i in range(2):
        out[i, 0, 2] = (-mo[1, i].astype(F32).T).astype(BF16)
    reduce_last(2)
    for n in range(SENDS):
        await_tiles([ssem.at[n], load[n]])


def body(amplitudes, cholesky, tile_mask):
    vec = cholesky[:, 0]
    vmem = pl.BlockSpec(memory_space=pltpu.VMEM)
    tile = (128, 128)
    return pl.pallas_call(
        kernel,
        out_shape=jax.ShapeDtypeStruct((2, 1, 4) + tile, BF16),
        in_specs=[pl.BlockSpec(memory_space=pltpu.SMEM), vmem, vmem],
        out_specs=vmem,
        scratch_shapes=[
            pltpu.VMEM((2, 3) + tile, BF16),
            pltpu.VMEM((4, 2, 4, 3) + tile, BF16),
            pltpu.VMEM((4, 2, 2, 4, 3) + tile, BF16),
            pltpu.VMEM((3, 4, 2, 2, 4) + tile, BF16),
            pltpu.VMEM((2, 2) + tile, BF16),
            pltpu.VMEM((3, 256, 1280), BF16),
            pltpu.VMEM((3, 2, 4, 4) + tile, BF16),
            pltpu.VMEM((3, 3, 4) + tile, BF16),
            pltpu.VMEM((3, 3, 4) + tile, BF16),
            pltpu.VMEM((3, 4) + tile, BF16),
            pltpu.VMEM((3, 4) + tile, BF16),
            pltpu.VMEM((3, 4) + tile, BF16),
            pltpu.VMEM((3, 4) + tile, BF16),
            pltpu.VMEM((2, 2) + tile, BF16),
            pltpu.VMEM((2, 2) + tile, BF16),
            pltpu.VMEM((3, 4) + tile, BF16),
            pltpu.VMEM((3, 4) + tile, BF16),
            pltpu.VMEM((3, 4) + tile, BF16),
            pltpu.VMEM((3, 4) + tile, BF16),
            pltpu.VMEM((256,) + tile, BF16),
            pltpu.SemaphoreType.DMA((SENDS,)),
            pltpu.SemaphoreType.DMA((RECVS,)),
            pltpu.SemaphoreType.DMA((LOCALS,)),
            pltpu.SemaphoreType.DMA((24,)),
        ],
        compiler_params=pltpu.CompilerParams(
            collective_id=0, has_side_effects=True, vmem_limit_bytes=56 * 1024 * 1024
        ),
    )(tile_mask.T, vec, amplitudes)


def solution(mesh):
    in_specs = (
        P("row", "col", None, None, None),
        P("row", "col", None, None, None),
        P("row", "col"),
    )
    out_specs = P("row", "col", None, None, None)
    return jax.shard_map(
        body, mesh=mesh, in_specs=in_specs, out_specs=out_specs, check_vma=False
    )
```

```python
import math

import jax
import jax.numpy as jnp
from jax import lax
from jax.experimental import pallas as pl
from jax.experimental.pallas import tpu as pltpu
from jax.sharding import PartitionSpec as P

MESH = pl.DeviceIdType.MESH
BF16 = jnp.bfloat16
F32 = jnp.float32
SENDS = 6
RECVS = 88
LOCALS = 6


def kernel(
    mask, lin, t_in, out, t, zl, yl, ag, mt, g, ob, rz, rx, s0, s1, f0, f1, fo, mo,
    qz, qx, cz, cx, size, ssem, rsem, lsem, xsem,
):
    r = lax.axis_index("row")
    col = lax.axis_index("col")
    y, k = lax.div(r, 2), lax.rem(r, 2)
    z, x = lax.div(col, 4), lax.rem(col, 4)

    def ring(v):
        return v, lax.rem(v + 3, 4), lax.rem(v + 1, 4), lax.rem(v + 2, 4)

    xs, ys, zs = ring(x), ring(y), ring(z)

    def dev(x_=x, y_=y, z_=z, k_=k):
        return (2 * y_ + k_, 4 * z_ + x_)

    to_x = [dev(x_=v) for v in xs]
    to_y = [dev(y_=v) for v in ys]
    to_z = [dev(z_=v) for v in zs]
    partner = dev(k_=1 - k)

    used = {"recv": 0, "local": 0, "swap": 0}
    load = [0] * SENDS

    def arrival():
        used["recv"] += 1
        return [rsem.at[used["recv"] - 1], 0]

    def await_tiles(due):
        blk = size.at[pl.ds(0, due[1])]
        pltpu.make_async_copy(blk, blk, due[0]).wait()

    def send(src, dst, to, group, due=None):
        due = due or arrival()
        tiles = math.prod(src.shape) // (128 * 128)
        due[1] += tiles
        load[group] += tiles
        pltpu.make_async_remote_copy(
            src_ref=src,
            dst_ref=dst,
            send_sem=ssem.at[group],
            recv_sem=due[0],
            device_id=to,
            device_id_type=MESH,
        ).start()
        return due

    def copy(src, dst):
        cp = pltpu.make_async_copy(src, dst, lsem.at[used["local"]])
        used["local"] += 1
        cp.start()
        return cp

    def mirror_of(i):
        return (y == z) & (x == 2 * k + i), dev(
            x_=2 * k + i, y_=z, z_=y, k_=lax.div(x, 2)
        )

    def exchange(src, dst):
        plans = []
        n = used["swap"]
        used["swap"] += 6
        slot = lax.rem(x, 2)
        for i in range(2):
            same, to = mirror_of(i)

            def remote(lands, i=i, to=to):
                return pltpu.make_async_remote_copy(
                    src_ref=src(i),
                    dst_ref=dst(lands),
                    send_sem=xsem.at[n + i],
                    recv_sem=xsem.at[n + 2 + lands],
                    device_id=to,
                    device_id_type=MESH,
                )

            here = pltpu.make_async_copy(src(i), dst(i), xsem.at[n + 4 + i])
            plans.append((same, remote(slot), remote(i), here))
        for same, there, back, here in plans:
            pl.when(jnp.logical_not(same))(there.start)
            pl.when(same)(here.start)
        return plans

    def exchange_wait(plans):
        for same, there, back, here in plans:

            def both(there=there, back=back):
                there.wait_send()
                back.wait_recv()

            pl.when(jnp.logical_not(same))(both)
            pl.when(same)(here.wait)

    barrier = pltpu.get_barrier_semaphore()

    def greet(to):
        pl.semaphore_signal(barrier, inc=1, device_id=to, device_id_type=MESH)

    selfs = jnp.int32(0)
    for i in range(2):
        same, to = mirror_of(i)
        selfs = selfs + jnp.where(same, 1, 0)
        pl.when(jnp.logical_not(same))(lambda to=to: greet(to))
    near = to_z[1:] + to_x[1:] + to_y[1:3] + [partner]
    for to in near:
        greet(to)
    mine = copy(lin.at[:, pl.ds(2 * x, 2)], zl.at[z, :, x, pl.ds(0, 2)])
    mine_h = copy(lin.at[:, 8 + lax.div(x, 2)], zl.at[z, :, x, 2])
    for i in range(2):
        flag = mask[0, i].astype(F32)
        for p in range(4):
            tile = (t_in[i, 0, p].astype(F32) * flag).astype(BF16)
            if p:
                t[i, p - 1] = tile
            else:
                ag[0, y, k, i, x] = tile
    mine.wait()
    mine_h.wait()
    pl.semaphore_wait(barrier, len(near) + 2 - selfs)

    class Gather:
        def __init__(self, p, y_first):
            self.p = p
            self.y_first = y_first
            self.one, self.two = (to_y, to_x) if y_first else (to_x, to_y)
            self.near = [None] * 4
            self.far = arrival()
            self.other = arrival()

        def block(self, n, m, rows=slice(None)):
            a, b = (n, m) if self.y_first else (m, n)
            return ag.at[self.p, ys[a], k, rows, xs[b]]

        def spread_second(self, n):
            blk = self.block(n, 0)
            self.near[n] = [
                send(blk, blk, self.two[2], 3),
                send(blk, blk, self.two[1], 3),
            ]

        def start(self):
            blk = self.block(0, 0)
            self.first = [send(blk, blk, self.one[2], 3), send(blk, blk, self.one[1], 3)]
            self.first.append(arrival())

        def middle(self):
            for n, row, m in ((1, 0, 2), (2, 1, 1)):
                await_tiles(self.first[n - 1])
                blk = self.block(n, 0, row)
                send(blk, blk, self.one[m], 3, self.first[2])
                self.spread_second(n)

        def across(self):
            await_tiles(self.first[2])
            self.spread_second(3)
            self.hand_over(0)

        def forward(self, n):
            for b, row, m in ((1, 0, 2), (2, 1, 1)):
                await_tiles(self.near[n][b - 1])
                blk = self.block(n, b, row)
                send(blk, blk, self.two[m], 3, self.far)

        def hand_over(self, m):
            if self.y_first:
                blk = ag.at[self.p, :, k, :, xs[m]]
            else:
                blk = ag.at[self.p, ys[m], k]
            send(blk, blk, partner, 4, self.other)

        def hand_near(self):
            self.hand_over(1)
            self.hand_over(2)

        def hand_far(self):
            await_tiles(self.far)
            self.hand_over(3)

        def done(self):
            await_tiles(self.other)

    a0, a1, a2 = (Gather(p, True) for p in range(3))

    a0.start()
    def swap(q):
        swaps.append(exchange(lambda i: t.at[i, q], lambda i: mt.at[q - 1, i]))

    swaps = []
    swap(1)

    def form(p):
        own, other = ((0, 0), (2, 1))[p - 1]
        exchange_wait(swaps[p - 1])
        for i in range(2):
            diff = t[i, own].astype(F32) - mt[other, i].astype(F32).T
            ag[p, y, k, i, x] = diff.astype(BF16)

    spread = [None] * 4
    for n, m in ((1, 2), (2, 1), (3, 3)):
        v = xs[m]
        spread[n] = arrival()
        src = lin.at[:, pl.ds(2 * v, 2)]
        send(src, zl.at[z, :, x, pl.ds(0, 2)], to_x[m], 0, spread[n])
        src = lin.at[:, 8 + lax.div(v, 2)]
        send(src, zl.at[z, :, x, 2], to_x[m], 0, spread[n])

    zc, yc, yp = [None] * 4, [None] * 4, [None] * 4
    depth = (3, 2, 2, 3)
    own_copies = []

    def z_send(j):
        src = zl.at[z, :, xs[j]]
        zc[j] = [send(src, src, to_z[2], 0), send(src, src, to_z[1], 0), arrival()]

    def z_forward(j):
        for n, row, m in ((1, 0, 2), (2, 1, 1)):
            await_tiles(zc[j][n - 1])
            blk = zl.at[zs[n], row, xs[j]]
            send(blk, blk, to_z[m], 0, zc[j][2])

    def y_block(j, n, rows=slice(None)):
        return yl.at[ys[n], k, rows, xs[j], pl.ds(0, depth[j])]

    def y_send(j):
        src = zl.at[z, :, xs[j], pl.ds(0, depth[j])]
        dst = y_block(j, 0)
        yc[j] = [send(src, dst, to_y[2], 1), send(src, dst, to_y[1], 1), arrival()]
        yp[j] = send(src, dst, partner, 2)
        own_copies.append(copy(src, dst))

    def y_forward(j):
        for n, row, m in ((1, 0, 2), (2, 1, 1)):
            await_tiles(yc[j][n - 1])
            blk = y_block(j, n, row)
            send(blk, blk, to_y[m], 1, yc[j][2])
            blk = y_block(j, n)
            send(blk, blk, partner, 2, yp[j])

    def y_finish(j):
        await_tiles(yc[j][2])
        blk = y_block(j, 3)
        send(blk, blk, partner, 2, yp[j])

    half = lax.rem(x, 2)
    red, relay, last = {}, {}, {}

    def lhs_of(q):
        rows = [
            jnp.concatenate(
                [zl[dz, i, dx, q] for dz in range(4) for dx in range(4)], axis=1
            )
            for i in range(2)
        ]
        return jnp.concatenate(rows, axis=0)

    def rhs_of(p, columns):
        rows = [
            jnp.concatenate(
                [ag[p, d // 4, d % 4 // 2, d % 2, c] for c in columns], axis=1
            )
            for d in range(16)
        ]
        return jnp.concatenate(rows, axis=0)

    def first_half(p, q):
        if q < 2:
            g[p, :, q * 512 : (q + 1) * 512] = jnp.dot(
                lhs_of(q), rhs_of(p, range(4)), preferred_element_type=F32
            ).astype(BF16)
        else:
            g[p, :, 1024:1280] = jnp.dot(
                lhs_of(2), rhs_of(p, (half, half + 2)), preferred_element_type=F32
            ).astype(BF16)

    def second_half(p, n):
        ay = zs[n]

        def tile_pair(ak, carry):
            rows = []
            for i in range(2):
                tiles = [yl[ay, ak, i, c, q] for q in range(2) for c in range(4)]
                tiles += [yl[ay, ak, i, half + 2 * c, 2] for c in range(2)]
                rows.append(jnp.concatenate(tiles, axis=1))
            right = jnp.concatenate(rows, axis=0)
            res = lax.dot_general(
                g[p],
                right,
                (((1,), (1,)), ((), ())),
                preferred_element_type=F32,
            ).astype(BF16)
            for i in range(2):
                for n in range(2):
                    ob[p, i, ay, 2 * ak + n] = res[
                        i * 128 : (i + 1) * 128, n * 128 : (n + 1) * 128
                    ]
            return carry

        lax.fori_loop(0, 2, tile_pair, 0)
        if p not in red:
            red[p] = [arrival(), arrival()]
            relay[p] = [arrival(), arrival()]
        lo, hi = pl.ds(0, 2), pl.ds(2, 2)
        row = ob.at[p, 0, ay]
        if n == 3:
            send(row.at[lo], qz.at[p, lo], to_z[2], 5, relay[p][0])
            send(row.at[hi], qz.at[p, hi], to_z[1], 5, relay[p][0])
        elif n == 2:
            send(row.at[hi], rz.at[p, 1, hi], to_z[2], 5, red[p][0])
        elif n == 1:
            send(row.at[lo], rz.at[p, 2, lo], to_z[1], 5, red[p][0])
        else:
            rz[p, 0] = ob[p, 0, z]
        up = n in (3, 1)
        tile = ob.at[p, 1, ay]
        send(tile.at[xs[3]], qx.at[p, ay], to_x[2 if up else 1], 5, relay[p][1])
        if up:
            send(tile.at[xs[1]], rx.at[p, 2, ay], to_x[1], 5, red[p][1])
        else:
            send(tile.at[xs[2]], rx.at[p, 1, ay], to_x[2], 5, red[p][1])
        rx[p, 0, ay] = ob[p, 1, ay, x]

    def reduce_relayed(p):
        await_tiles(relay[p][0])
        for n, m, part in ((2, 1, slice(0, 2)), (1, 2, slice(2, 4))):
            both = ob[p, 0, zs[n], part].astype(F32) + qz[p, part].astype(F32)
            cz[p, part] = both.astype(BF16)
            part = pl.ds(part.start, 2)
            send(cz.at[p, part], rz.at[p, m, part], to_z[n], 5, red[p][0])
        await_tiles(relay[p][1])
        for n in (3, 1, 2, 0):
            b, m = (2, 1) if n in (3, 1) else (1, 2)
            at = zs[n]
            both = ob[p, 1, at, xs[b]].astype(F32) + qx[p, at].astype(F32)
            cx[p, at] = both.astype(BF16)
            send(cx.at[p, at], rx.at[p, m, at], to_x[b], 5, red[p][1])

    def total(ref, p):
        acc = ref[p, 0].astype(F32)
        for n in range(1, ref.shape[1]):
            acc = acc + ref[p, n].astype(F32)
        return acc.astype(BF16)

    def reduce_first(p):
        last[p] = [arrival(), arrival()]
        await_tiles(red[p][0])
        s0[p] = total(rz, p)
        for n in (3, 1, 2):
            send(s0.at[p, xs[n]], f0.at[p, x], to_x[n], 5, last[p][0])
        f0[p, x] = s0[p, x]
        await_tiles(red[p][1])
        s1[p] = total(rx, p)
        for n in (3, 1, 2):
            send(s1.at[p, zs[n]], f1.at[p, z], to_z[n], 5, last[p][1])
        f1[p, z] = s1[p, z]

    def reduce_last(p):
        for i, ref in enumerate((f0, f1)):
            await_tiles(last[p][i])
            tile = total(ref, p)
            if p:
                out[i, 0, (1, 3)[p - 1]] = tile
            if p < 2:
                fo[p, i] = tile

    z_send(0)
    y_send(0)
    a0.spread_second(0)
    a0.middle()
    swap(2)
    a0.across()
    y_forward(0)
    z_forward(0)
    await_tiles(spread[1])
    z_send(1)
    y_send(1)
    await_tiles(spread[2])
    z_send(2)
    y_send(2)
    await_tiles(spread[3])
    z_send(3)
    a0.forward(0)
    form(1)
    a1.start()
    a1.spread_second(0)
    form(2)
    a2.start()
    y_send(3)
    a0.forward(1)
    a0.forward(2)
    y_forward(1)
    z_forward(1)
    a1.middle()
    a2.spread_second(0)
    a2.middle()
    y_forward(2)
    a0.forward(3)
    a1.across()
    a2.across()
    z_forward(2)
    a0.hand_near()
    y_finish(0)
    y_finish(1)
    a0.hand_far()
    z_forward(3)
    y_forward(3)
    y_finish(2)
    a1.forward(0)
    a1.forward(1)
    a1.forward(2)
    a1.forward(3)
    a1.hand_near()
    a2.forward(0)
    for j in range(4):
        await_tiles(zc[j][2])
    a0.done()
    first_half(0, 0)
    y_finish(3)
    a2.forward(1)
    a2.forward(2)
    first_half(0, 1)
    a1.hand_far()
    a2.forward(3)
    a2.hand_near()
    first_half(0, 2)
    for j in range(4):
        await_tiles(yp[j])
    for cp in own_copies:
        cp.wait()
    second_half(0, 3)
    second_half(0, 1)
    a2.hand_far()
    second_half(0, 2)
    second_half(0, 0)
    a1.done()
    for q in range(3):
        first_half(1, q)
    reduce_relayed(0)
    for n in (3, 1, 2, 0):
        second_half(1, n)
    reduce_first(0)
    a2.done()
    first_half(2, 0)
    first_half(2, 1)
    reduce_relayed(1)
    first_half(2, 2)
    reduce_last(0)
    back0 = exchange(lambda i: fo.at[0, i], lambda i: mo.at[0, i])
    second_half(2, 3)
    second_half(2, 1)
    second_half(2, 2)
    second_half(2, 0)
    reduce_first(1)
    reduce_relayed(2)
    reduce_last(1)
    back1 = exchange(lambda i: fo.at[1, i], lambda i: mo.at[1, i])
    reduce_first(2)
    exchange_wait(back0)
    for i in range(2):
        diff = fo[0, i].astype(F32) - mo[0, i].astype(F32).T
        out[i, 0, 0] = diff.astype(BF16)
    exchange_wait(back1)
    for i in range(2):
        out[i, 0, 2] = (-mo[1, i].astype(F32).T).astype(BF16)
    reduce_last(2)
    for n in range(SENDS):
        await_tiles([ssem.at[n], load[n]])


def body(amplitudes, cholesky, tile_mask):
    vec = cholesky[:, 0]
    vmem = pl.BlockSpec(memory_space=pltpu.VMEM)
    tile = (128, 128)
    return pl.pallas_call(
        kernel,
        out_shape=jax.ShapeDtypeStruct((2, 1, 4) + tile, BF16),
        in_specs=[pl.BlockSpec(memory_space=pltpu.SMEM), vmem, vmem],
        out_specs=vmem,
        scratch_shapes=[
            pltpu.VMEM((2, 3) + tile, BF16),
            pltpu.VMEM((4, 2, 4, 3) + tile, BF16),
            pltpu.VMEM((4, 2, 2, 4, 3) + tile, BF16),
            pltpu.VMEM((3, 4, 2, 2, 4) + tile, BF16),
            pltpu.VMEM((2, 2) + tile, BF16),
            pltpu.VMEM((3, 256, 1280), BF16),
            pltpu.VMEM((3, 2, 4, 4) + tile, BF16),
            pltpu.VMEM((3, 3, 4) + tile, BF16),
            pltpu.VMEM((3, 3, 4) + tile, BF16),
            pltpu.VMEM((3, 4) + tile, BF16),
            pltpu.VMEM((3, 4) + tile, BF16),
            pltpu.VMEM((3, 4) + tile, BF16),
            pltpu.VMEM((3, 4) + tile, BF16),
            pltpu.VMEM((2, 2) + tile, BF16),
            pltpu.VMEM((2, 2) + tile, BF16),
            pltpu.VMEM((3, 4) + tile, BF16),
            pltpu.VMEM((3, 4) + tile, BF16),
            pltpu.VMEM((3, 4) + tile, BF16),
            pltpu.VMEM((3, 4) + tile, BF16),
            pltpu.VMEM((256,) + tile, BF16),
            pltpu.SemaphoreType.DMA((SENDS,)),
            pltpu.SemaphoreType.DMA((RECVS,)),
            pltpu.SemaphoreType.DMA((LOCALS,)),
            pltpu.SemaphoreType.DMA((24,)),
        ],
        compiler_params=pltpu.CompilerParams(
            collective_id=0, has_side_effects=True, vmem_limit_bytes=56 * 1024 * 1024
        ),
    )(tile_mask.T, vec, amplitudes)


def solution(mesh):
    in_specs = (
        P("row", "col", None, None, None),
        P("row", "col", None, None, None),
        P("row", "col"),
    )
    out_specs = P("row", "col", None, None, None)
    return jax.shard_map(
        body, mesh=mesh, in_specs=in_specs, out_specs=out_specs, check_vma=False
    )
```
